32 devices in a mesh: view: 4 (over z), patch: 8 (over y, x, core).
Axes of the slice: x: 2, y: 2, z: 4, core: 2. Of those that a mesh axis runs over, the one named last changes fastest.
Arguments:
- coefficients: bfloat16 [8, 2304, 32, 512], P('view', 'patch'), may hold values from -0.1875 to 0.1875
- sky_year: bfloat16 [2304, 8760], P('patch'), may hold values from 0.19921875 to 5
- hour_list: int32 [96], replicated, may hold values from 0 to 8759
- retention: float32 [32, 512], P('patch'), may hold values from 0 to 1
Outputs:
- acuity: float32 [32, 8, 96, 512], P('patch', 'view')
- veil: float32 [32, 8, 96, 512], P('patch', 'view')
The draws below stay inside these ranges and needn't reach their ends.
All inputs are finite; a program needn't handle non-finite values.
Results may differ from the reference program's by a relative error of at most 0.0003.
Values may be sent and summed in bfloat16 or wider, within the bound.
A program may use at most 128 MiB of HBM per device.

```python
import math
import jax
import jax.numpy as jnp
from jax import lax

VIEWS = 8
PATCHES = 2304
COLS = 512
HOURS = 96
YEAR = 8760
STRIP_LINE_COUNT = 32


def draw_retention(key, part):
    key_rate, key_rough, marker_image_lines, key_depth = jax.random.split(key, 4)
    spread = jax.random.uniform(key_rate, (COLS,), jnp.float32, math.log(0.3), math.log(40.0))
    strength = jnp.exp(spread)
    roughness = jax.random.uniform(key_rough, (STRIP_LINE_COUNT, COLS), jnp.float32, 0.5, 1.5)
    dazzle_spike_lines = jax.random.randint(marker_image_lines, (3,), 0, STRIP_LINE_COUNT)
    sample_locations = jnp.arange(STRIP_LINE_COUNT, dtype=jnp.int32)
    lit_sample_spots = jnp.any(sample_locations[:, None] == dazzle_spike_lines[None, :], axis=1)
    depths = jax.random.uniform(key_depth, (STRIP_LINE_COUNT, COLS), jnp.float32, 0.5, 0.8)
    factor = jnp.where(lit_sample_spots[:, None], depths, jnp.float32(1.0))
    return jnp.exp(-strength[None, :] * roughness / STRIP_LINE_COUNT) * factor


def place_ends(array, stream_key, low, top_value):
    shape = array.shape
    index_at = [jax.random.randint(jax.random.fold_in(stream_key, axis), (), 0, shape[axis]) for axis in range(len(shape))]
    array = array.at[tuple(index_at)].set(low)
    longest = shape.index(max(shape))
    index_at[longest] = (index_at[longest] + 1) % shape[longest]
    return array.at[tuple(index_at)].set(top_value)


def with_spikes(drawn, own_key, source, target, shards_of, factor):
    owner, partner = [(jnp.arange(drawn.shape[axis_at]) // (drawn.shape[axis_at] // shards_of)).reshape([-1 if axis == axis_at else 1 for axis in range(drawn.ndim)]) for axis_at in (source, target)]
    chosen = jax.random.permutation(own_key, shards_of)[partner]
    strong = (owner == chosen) | (owner == (partner + shards_of // 2) % shards_of)
    return jnp.where(strong, factor * drawn, drawn)


def levels(own_key, shape, cuts, smallest, high):
    level, own = 1.0, jax.random.fold_in(own_key, 6)
    for dim, parts in cuts:
        draws = jnp.exp(jax.random.uniform(jax.random.fold_in(own, dim), (parts,), jnp.float32, smallest / len(cuts), high / len(cuts)))
        level = level * jnp.repeat(draws, shape[dim] // parts).reshape([-1 if axis == dim else 1 for axis in range(len(shape))])
    return level


def heavy_noise(key, extent, scale, limit, cuts, heavy, held_as=jnp.bfloat16):
    values = scale * jax.random.normal(key, extent, jnp.float32)
    if cuts:
        values = values * levels(key, extent, cuts, -0.22, 0.18)
    return jnp.clip(with_spikes(values, jax.random.fold_in(key, 3), *heavy), -limit, limit).astype(held_as)


def setup_inputs(seed: int = 0) -> dict:
    arg_keys = jax.random.split(jax.random.key(seed), 5)
    coefficients = heavy_noise(arg_keys[0], (VIEWS, PATCHES, STRIP_LINE_COUNT, COLS), PATCHES ** -0.5, 0.1875, ((0, 4), (1, 8)), (1, 2, 8, 2.0))
    sky_year = jnp.clip(jnp.exp(math.log(5.0) - 3.2227897 * jax.random.uniform(arg_keys[1], (PATCHES, YEAR), jnp.float32) ** levels(arg_keys[1], (PATCHES, YEAR), ((0, 8),), -0.2, 0.2)), 0.19921875, 5.0).astype(jnp.bfloat16)
    hour_list = place_ends(jax.random.randint(arg_keys[2], (HOURS,), 0, YEAR), jax.random.fold_in(arg_keys[2], 1), 0, YEAR - 1).astype(jnp.int32)
    retention = draw_retention(jax.random.fold_in(arg_keys[4], 71), 0)
    return {"coefficients": coefficients, "sky_year": sky_year, "hour_list": hour_list, "retention": retention}


binomial_taps = (0.0625, 0.25, 0.375, 0.25, 0.0625)


def pascal_kernel(field, device_axis_name):
    size = field.shape[device_axis_name]
    widths = [(0, 0)] * field.ndim
    widths[device_axis_name] = (2, 2)
    padded = jnp.pad(field, widths)
    total = jnp.zeros_like(field)
    for offset in range(5):
        total = total + binomial_taps[offset] * lax.slice_in_dim(padded, offset, offset + size, axis=device_axis_name)
    return total


def reference(coefficients, sky_year, hour_list, retention):
    sky = jnp.take(sky_year, hour_list, axis=1)
    sky_rows = sky.T

    def render(single_view):
        flat = single_view.reshape(single_view.shape[0], -1)
        return jnp.dot(sky_rows, flat, preferred_element_type=jnp.float32).reshape(sky_rows.shape[0], single_view.shape[1], single_view.shape[2])

    images = lax.map(render, coefficients)
    luminance = jnp.transpose(images, (2, 0, 1, 3))
    across = pascal_kernel(luminance, 3)
    acuity = pascal_kernel(across, 0)

    def advance(state, inputs):
        carried = inputs[0][None, None, :] * state + inputs[1]
        return carried, carried

    initial_state = jnp.zeros(luminance.shape[1:], jnp.float32)
    _, forward = lax.scan(advance, initial_state, (retention, luminance))
    _, reverse_pass = lax.scan(advance, initial_state, (retention, luminance), reverse=True)
    veil = 0.125 * (forward + reverse_pass)
    return acuity, veil
```

```python
import jax
import jax.numpy as jnp
from jax import lax
from jax.experimental import pallas as pl
from jax.experimental.pallas import tpu as pltpu
from jax.sharding import PartitionSpec as P

binomial_taps = (0.0625, 0.25, 0.375, 0.25, 0.0625)
MESH = pl.DeviceIdType.MESH
LEVELS = 32767.0


def padded_2(block, sides, width):
    for axis, dim in sides:
        count = lax.axis_size(axis)
        forward = [(i, i + 1) for i in range(count - 1)]
        backward = [(target, source) for source, target in forward]
        low = lax.ppermute(
            lax.slice_in_dim(block, block.shape[dim] - width, None, axis=dim), axis, forward
        )
        high = lax.ppermute(lax.slice_in_dim(block, 0, width, axis=dim), axis, backward)
        block = jnp.concatenate([low, block, high], axis=dim)
    return block


def entering(value, axis, join, neutral, backward):
    count, mine = (lax.axis_size(axis), lax.axis_index(axis))
    pieces = jax.tree.map(lambda part: lax.all_gather(part, axis), value)
    if backward:
        pieces = jax.tree.map(lambda part: part[::-1], pieces)
        mine = count - 1 - mine
    running = jax.tree.map(
        lambda part, zero: jnp.full_like(part, 0) + jnp.asarray(zero, part.dtype), value, neutral
    )

    def hop(position, running):
        longer = join(running, jax.tree.map(lambda part: part[position], pieces))
        return jax.tree.map(lambda new, old: jnp.where(position < mine, new, old), longer, running)

    return lax.fori_loop(0, count - 1, hop, running)


def combine(earlier, later):
    return (earlier[0] * later[0], later[0] * earlier[1] + later[1])


def taps_sum(padded, axis, length):
    total = jnp.zeros(
        padded.shape[:axis] + (length,) + padded.shape[axis + 1 :],
        jnp.float32,
    )
    for offset in range(5):
        total = total + binomial_taps[offset] * lax.slice_in_dim(
            padded, offset, offset + length, axis=axis
        )
    return total


def general(coefficients, sky_year, hour_list, retention):
    sky_shard_values = jnp.take(sky_year, hour_list, axis=1)
    row_count = retention.shape[0]
    luminance = lax.psum_scatter(
        jnp.einsum(
            "ph,vprc->rvhc", sky_shard_values, coefficients, preferred_element_type=jnp.float32
        ),
        "patch",
        scatter_dimension=0,
        tiled=True,
    )
    padded = padded_2(luminance, (("patch", 0),), 2)
    image_width = padded.shape[3]
    wide_pad = jnp.pad(padded, ((0, 0), (0, 0), (0, 0), (2, 2)))
    across = taps_sum(wide_pad, 3, image_width)
    acuity = taps_sum(across, 0, row_count)
    retain_rates = retention[:, None, None, :]
    front_gain, front_sum = lax.associative_scan(combine, (retain_rates, luminance), axis=0)
    unity = (jnp.ones_like(front_gain[-1]), jnp.zeros_like(front_sum[-1]))
    _, incoming_down = entering((front_gain[-1], front_sum[-1]), "patch", combine, unity, False)
    forward = front_gain * incoming_down[None] + front_sum
    back_gain, back_sum = lax.associative_scan(
        combine, (retain_rates, luminance), reverse=True, axis=0
    )
    _, incoming_up = entering((back_gain[0], back_sum[0]), "patch", combine, unity, True)
    reverse_pass = back_gain * incoming_up[None] + back_sum
    veil = 0.125 * (forward + reverse_pass)
    return (acuity, veil)


TILE = 256
LANES = 128
GROUP = 4
SLOTS = 4


def encode(x):
    top = jnp.maximum(jnp.max(jnp.abs(x), axis=0, keepdims=True), 1e-30)
    level = jnp.round(x * (LEVELS / top))
    return level.astype(jnp.int32).astype(jnp.int16), top * (1.0 / LEVELS)


def decode(code, step):
    return code.astype(jnp.int32).astype(jnp.float32) * step


def kernel(
    hour_ref, year_ref, coef_ref, ret_ref, acu_out, veil_out,
    year, picks, spread, lhs, held, mine, given, taken,
    code_out, top_out, code_in, top_in, lum, across,
    halo_out, halo_top_out, halo_in, halo_top_in,
    carry_out, carry_top_out, carry_in, carry_top_in,
    rets, ends, acuity, veil,
    year_sem, load_sem, ret_sem, pair_sem, hop_sem, halo_sem, carry_sem, out_sem, local_sem,
):
    view = lax.axis_index("view")
    me = lax.axis_index("patch")
    devices = 8
    chips = 4
    core = me % 2
    chip = me // 2
    cx = chip % 2
    cy = chip // 2
    other = 1 - core
    partner = chip * 2 + other
    hours = hour_ref.shape[1]
    depth = year_ref.shape[0]
    rows, _, columns = acuity.shape
    half = rows // 2
    tiles = columns // TILE
    groups = rows // GROUP

    def at(target):
        return (view, target)

    def chip_of(k, owner):
        fx = (1 - owner) * (1 - k // 2) + owner * (1 - k % 2)
        fy = owner * (1 - k // 2) + (1 - owner) * (1 - k % 2)
        return 2 * (cy + fy * (1 - 2 * cy)) + cx + fx * (1 - 2 * cx)

    def remote(src, dst, send, recv, target):
        return pltpu.make_async_remote_copy(
            src_ref=src, dst_ref=dst, send_sem=send, recv_sem=recv,
            device_id=at(target), device_id_type=MESH,
        )

    units = [
        (0, 0, other), (0, 0, core), (1, 0, other), (1, 0, core),
        (2, 0, other), (2, 0, core), (0, 1, other), (0, 1, core),
        (1, 1, other), (1, 1, core), (2, 1, other), (2, 1, core),
        (3, 0, other), (3, 0, core), (3, 1, other), (3, 1, core),
    ]

    def load(u):
        k, t, v = units[u]
        slot = u % SLOTS
        return [
            pltpu.make_async_copy(
                coef_ref.at[v, :, chip_of(k, v), t * (TILE // LANES) + j, s],
                held.at[slot, s, j],
                load_sem.at[slot, s * (TILE // LANES) + j],
            )
            for s in range(groups)
            for j in range(TILE // LANES)
        ]

    table = pltpu.make_async_copy(year_ref, year, year_sem)
    table.start()
    for u in range(SLOTS):
        for copy in load(u):
            copy.start()

    barrier = pltpu.get_barrier_semaphore()
    for step in range(1, devices):
        pl.semaphore_signal(
            barrier, inc=1, device_id=at((me + step) % devices), device_id_type=MESH
        )

    days = year_ref.shape[1]
    picks[...] = jnp.where(
        lax.broadcasted_iota(jnp.int32, (days, hours), 0) == hour_ref[...], 1.0, 0.0
    ).astype(jnp.bfloat16)
    wide_shape = (depth, depth * GROUP)
    spread[...] = jnp.where(
        lax.broadcasted_iota(jnp.int32, wide_shape, 1) // GROUP
        == lax.broadcasted_iota(jnp.int32, wide_shape, 0),
        1.0,
        0.0,
    ).astype(jnp.bfloat16)
    rets[me] = ret_ref[...]

    pl.semaphore_wait(barrier, devices - 1)

    ret_copies = []
    for step in range(1, devices):
        target = (me + step) % devices
        copy = remote(
            ret_ref, rets.at[me], ret_sem.at[0, step], ret_sem.at[1, step], target
        )
        copy.start()
        ret_copies.append(copy)

    table.wait()
    sky = jnp.dot(year[...], picks[...], preferred_element_type=jnp.float32).T
    wide = jnp.dot(sky.astype(jnp.bfloat16), spread[...], preferred_element_type=jnp.float32)
    place = lax.broadcasted_iota(jnp.int32, (hours, depth * GROUP), 1) % GROUP
    for r in range(GROUP):
        lhs[r * hours : (r + 1) * hours, :] = jnp.where(place == r, wide, 0.0).astype(jnp.bfloat16)

    def pair(k, t):
        i = k * tiles + t
        return remote(
            given.at[k, t], taken.at[k, t], pair_sem.at[0, i], pair_sem.at[1, i], partner
        )

    def run(u):
        k, t, v = units[u]
        slot = u % SLOTS
        dst = mine if u % 2 else given
        for copy in load(u):
            copy.wait()

        @pl.loop(0, groups)
        def _(s):
            block = jnp.concatenate(
                [
                    held[slot, s, j].reshape(depth * GROUP, LANES)
                    for j in range(TILE // LANES)
                ],
                axis=1,
            )
            dst[k, t, pl.ds(s * GROUP, GROUP)] = jnp.dot(
                lhs[...], block, preferred_element_type=jnp.float32
            ).reshape(GROUP, hours, TILE)

        if u % 2 == 0:
            pair(k, t).start()
        if u + SLOTS < len(units):
            for copy in load(u + SLOTS):
                copy.start()

    def hop(k, t):
        i = k * tiles + t
        target = chip_of(2 if k == 2 else 1, core) * 2 + core
        return [
            remote(code_out.at[k, t], code_in.at[k, t], hop_sem.at[0, 0, i], hop_sem.at[1, 0, i], target),
            remote(top_out.at[k, t], top_in.at[k, t], hop_sem.at[0, 1, i], hop_sem.at[1, 1, i], target),
        ]

    def first(k, t):
        pair(k, t).wait_recv()

        @pl.loop(0, rows, unroll=2)
        def _(r):
            code_out[k, t, r], top_out[k, t, r] = encode(mine[k, t, r] + taken[k, t, r])

        for copy in hop(k, t):
            copy.start()

    def second(t):
        pair(2, t).wait_recv()
        for copy in hop(0, t):
            copy.wait_recv()

        @pl.loop(0, rows, unroll=2)
        def _(r):
            came = decode(code_in[0, t, r], top_in[0, t, r])
            code_out[2, t, r], top_out[2, t, r] = encode(mine[2, t, r] + taken[2, t, r] + came)

        for copy in hop(2, t):
            copy.start()

    def gather(t):
        pair(3, t).wait_recv()
        for copy in hop(1, t):
            copy.wait_recv()

        @pl.loop(0, rows, unroll=2)
        def _(r):
            came = decode(code_in[1, t, r], top_in[1, t, r])
            mine[3, t, r] = mine[3, t, r] + taken[3, t, r] + came

    not_last = chip < chips - 1
    not_first = chip > 0

    def span(t):
        return pl.ds(t * TILE, TILE)

    def rate(r, t):
        return rets[chip * 2 + r // half, pl.ds(r % half, 1), span(t)]

    def halo(way, t):
        i = way * tiles + t
        target = (chip + (1 - 2 * way) + chips) % chips * 2 + core
        return [
            remote(halo_out.at[way, t], halo_in.at[way, t], halo_sem.at[0, 0, i], halo_sem.at[1, 0, i], target),
            remote(halo_top_out.at[way, t], halo_top_in.at[way, t], halo_sem.at[0, 1, i], halo_sem.at[1, 1, i], target),
        ]

    def carry(way, t, target):
        i = target * tiles + t
        j = chip * tiles + t
        return [
            remote(carry_out.at[way, t], carry_in.at[chip, t], carry_sem.at[0, 0, i], carry_sem.at[1, 0, j], target * 2 + core),
            remote(carry_top_out.at[way, t], carry_top_in.at[chip, t], carry_sem.at[0, 1, i], carry_sem.at[1, 1, j], target * 2 + core),
        ]

    def arrival(source, t):
        i = source * tiles + t
        return [
            remote(carry_out.at[0, t], carry_in.at[source, t], carry_sem.at[0, 0, i], carry_sem.at[1, 0, i], source * 2 + core),
            remote(carry_top_out.at[0, t], carry_top_in.at[source, t], carry_sem.at[0, 1, i], carry_sem.at[1, 1, i], source * 2 + core),
        ]

    part = 32

    def finish(t):
        for copy in hop(2, t):
            copy.wait_recv()

        @pl.loop(0, hours // part)
        def _(b):
            span_h = pl.ds(pl.multiple_of(b * part, part), part)
            state = jnp.zeros((part, TILE), jnp.float32)
            for r in range(rows):
                row = mine[3, t, r, span_h, :] + decode(code_in[2, t, r, span_h, :], top_in[2, t, r])
                lum[r + 2, span_h, span(t)] = row
                state = rate(r, t) * state + row
                mine[0, t, r, span_h, :] = state
            ends[0, span_h, :] = state
            state = jnp.zeros((part, TILE), jnp.float32)
            for r in range(rows - 1, -1, -1):
                state = rate(r, t) * state + lum[r + 2, span_h, span(t)]
                mine[0, t, r, span_h, :] = mine[0, t, r, span_h, :] + state
            ends[1, span_h, :] = state

        @pl.when(not_last)
        def _():
            carry_out[0, t], carry_top_out[0, t] = encode(ends[0])
            for i in range(2):
                halo_out[0, t, i], halo_top_out[0, t, i] = encode(lum[rows + i, :, span(t)])
            for copy in halo(0, t):
                copy.start()

        @pl.when(not_first)
        def _():
            carry_out[1, t], carry_top_out[1, t] = encode(ends[1])
            for i in range(2):
                halo_out[1, t, i], halo_top_out[1, t, i] = encode(lum[2 + i, :, span(t)])
            for copy in halo(1, t):
                copy.start()

        for target in range(chips):
            @pl.when(target > chip)
            def _():
                for copy in carry(0, t, target):
                    copy.start()

            @pl.when(target < chip)
            def _():
                for copy in carry(1, t, target):
                    copy.start()

    def gain(source, t):
        total = rets[source * 2, 0:1, span(t)]
        for r in range(1, rows):
            total = total * rets[source * 2 + r // half, r % half : r % half + 1, span(t)]
        return total

    def stay(i, t):
        src, dst = ((acuity, acu_out), (veil, veil_out))[i]
        return pltpu.make_async_copy(
            src.at[pl.ds(core * half, half), :, span(t)],
            dst.at[:, core, :, span(t)],
            local_sem.at[i, t],
        )

    def leave(i, t):
        src, dst = ((acuity, acu_out), (veil, veil_out))[i]
        return remote(
            src.at[pl.ds(other * half, half), :, span(t)],
            dst.at[:, core, :, span(t)],
            out_sem.at[0, i, t],
            out_sem.at[1, i, t],
            partner,
        )

    def glare(t):
        ends[0] = jnp.zeros((hours, TILE), jnp.float32)
        ends[1] = jnp.zeros((hours, TILE), jnp.float32)
        for source in range(chips):
            @pl.when(source < chip)
            def _():
                for copy in arrival(source, t):
                    copy.wait_recv()
                ends[0] = gain(source, t) * ends[0] + decode(carry_in[source, t], carry_top_in[source, t])

        for source in range(chips - 1, -1, -1):
            @pl.when(source > chip)
            def _():
                for copy in arrival(source, t):
                    copy.wait_recv()
                ends[1] = gain(source, t) * ends[1] + decode(carry_in[source, t], carry_top_in[source, t])

        above = []
        total = None
        for r in range(rows):
            total = rate(r, t) if total is None else total * rate(r, t)
            above.append(total)
        below = []
        total = None
        for r in range(rows - 1, -1, -1):
            total = rate(r, t) if total is None else total * rate(r, t)
            below.append(total)
        for r in range(rows):
            veil[r, :, span(t)] = 0.125 * (
                mine[0, t, r] + (above[r] * ends[0] + below[rows - 1 - r] * ends[1])
            )
        stay(1, t).start()
        leave(1, t).start()

    column = lax.broadcasted_iota(jnp.int32, (hours, columns), 1)

    def shifted(row, k):
        moved = pltpu.roll(row, (-k) % columns, 1)
        inside = column < columns - k if k > 0 else column >= -k
        return jnp.where(inside, moved, 0.0)

    def blur(row):
        return (
            binomial_taps[2] * row
            + binomial_taps[1] * (shifted(row, -1) + shifted(row, 1))
            + binomial_taps[0] * (shifted(row, -2) + shifted(row, 2))
        )

    for u in range(3):
        run(u)
    first(0, 0)
    run(3)
    run(4)
    first(1, 0)
    for u in range(5, 9):
        run(u)
    second(0)
    first(0, 1)
    run(9)
    run(10)
    first(1, 1)
    for u in range(11, 16):
        run(u)
    for copy in ret_copies:
        copy.wait()
    gather(0)
    finish(0)
    second(1)
    glare(0)
    gather(1)
    finish(1)

    @pl.loop(0, rows)
    def _(r):
        across[r] = blur(lum[r + 2])

    def down_taps(x0, x1, x2, x3, x4):
        return binomial_taps[2] * x2 + binomial_taps[1] * (x1 + x3) + binomial_taps[0] * (x0 + x4)

    @pl.loop(2, rows - 2)
    def _(r):
        acuity[r] = down_taps(*[across[r + k] for k in range(-2, 3)])

    zero = jnp.zeros((hours, columns), jnp.float32)

    def edge(way, place):
        for t in range(tiles):
            for copy in halo(way, t):
                copy.wait_recv()
        for i in range(2):
            row = jnp.concatenate(
                [decode(halo_in[way, t, i], halo_top_in[way, t, i]) for t in range(tiles)], axis=1
            )
            lum[place + i] = blur(row)

    @pl.when(not_first)
    def _():
        edge(0, 0)

    @pl.when(chip == 0)
    def _():
        for i in range(2):
            lum[i] = zero

    @pl.when(not_last)
    def _():
        edge(1, rows + 2)

    @pl.when(chip == chips - 1)
    def _():
        for i in range(2):
            lum[rows + 2 + i] = zero

    for r in (0, 1, rows - 2, rows - 1):
        acuity[r] = down_taps(
            *[
                across[s] if 0 <= s < rows else lum[s + 2]
                for s in range(r - 2, r + 3)
            ]
        )
    for t in range(tiles):
        stay(0, t).start()
        leave(0, t).start()

    glare(1)

    for k in range(chips):
        for t in range(tiles):
            pair(k, t).wait_send()
    for k in range(3):
        for t in range(tiles):
            for copy in hop(k, t):
                copy.wait_send()

    for t in range(tiles):
        @pl.when(not_last)
        def _():
            for copy in halo(0, t):
                copy.wait_send()

        @pl.when(not_first)
        def _():
            for copy in halo(1, t):
                copy.wait_send()

        for target in range(chips):
            @pl.when(target > chip)
            def _():
                for copy in carry(0, t, target):
                    copy.wait_send()

            @pl.when(target < chip)
            def _():
                for copy in carry(1, t, target):
                    copy.wait_send()

    for t in range(tiles):
        for i in range(2):
            stay(i, t).wait()
            leave(i, t).wait()


def fused(coefficients, sky_year, hour_list, retention):
    views, depth, all_rows, columns = coefficients.shape
    hours = hour_list.shape[0]
    half = retention.shape[0]
    rows = 2 * half
    chips = all_rows // rows
    groups = rows // GROUP
    tiles = columns // TILE
    f32, bf16, i16 = jnp.float32, jnp.bfloat16, jnp.int16
    grouped = coefficients.reshape(
        views, depth, chips, groups, GROUP, columns // LANES, LANES
    ).transpose(0, 1, 2, 5, 3, 4, 6)
    image = (rows, hours, columns)
    tile = (tiles, rows, hours, TILE)
    tops = (tiles, rows, 1, TILE)
    out = jax.ShapeDtypeStruct((half, views, hours, columns), f32)
    dma = pltpu.SemaphoreType.DMA
    return pl.pallas_call(
        kernel,
        out_shape=(out, out),
        in_specs=[
            pl.BlockSpec(memory_space=pltpu.VMEM),
            pl.BlockSpec(memory_space=pl.ANY),
            pl.BlockSpec(memory_space=pl.ANY),
            pl.BlockSpec(memory_space=pltpu.VMEM),
        ],
        out_specs=[pl.BlockSpec(memory_space=pl.ANY)] * 2,
        scratch_shapes=[
            pltpu.VMEM(sky_year.shape, bf16),
            pltpu.VMEM((sky_year.shape[1], hours), bf16),
            pltpu.VMEM((depth, depth * GROUP), bf16),
            pltpu.VMEM((GROUP * hours, depth * GROUP), bf16),
            pltpu.VMEM((SLOTS, groups, TILE // LANES, depth, GROUP, LANES), bf16),
            pltpu.VMEM((chips,) + tile, f32),
            pltpu.VMEM((chips,) + tile, f32),
            pltpu.VMEM((chips,) + tile, f32),
            pltpu.VMEM((3,) + tile, i16),
            pltpu.VMEM((3,) + tops, f32),
            pltpu.VMEM((3,) + tile, i16),
            pltpu.VMEM((3,) + tops, f32),
            pltpu.VMEM((rows + 4, hours, columns), f32),
            pltpu.VMEM(image, f32),
            pltpu.VMEM((2, tiles, 2, hours, TILE), i16),
            pltpu.VMEM((2, tiles, 2, 1, TILE), f32),
            pltpu.VMEM((2, tiles, 2, hours, TILE), i16),
            pltpu.VMEM((2, tiles, 2, 1, TILE), f32),
            pltpu.VMEM((2, tiles, hours, TILE), i16),
            pltpu.VMEM((2, tiles, 1, TILE), f32),
            pltpu.VMEM((chips, tiles, hours, TILE), i16),
            pltpu.VMEM((chips, tiles, 1, TILE), f32),
            pltpu.VMEM((2 * chips, half, columns), f32),
            pltpu.VMEM((2, hours, TILE), f32),
            pltpu.VMEM(image, f32),
            pltpu.VMEM(image, f32),
            dma,
            dma((SLOTS, groups * (TILE // LANES))),
            dma((2, 2 * chips)),
            dma((2, chips * tiles)),
            dma((2, 2, 3 * tiles)),
            dma((2, 2, 2 * tiles)),
            dma((2, 2, chips * tiles)),
            dma((2, 2, tiles)),
            dma((2, tiles)),
        ],
        compiler_params=pltpu.CompilerParams(
            collective_id=0, has_side_effects=True, vmem_limit_bytes=56 * 1024 * 1024
        ),
    )(hour_list.reshape(1, hours), sky_year, grouped, retention)


def solution(mesh):
    size = mesh.shape["patch"]

    def shards(coefficients, sky_year, hour_list, retention):
        square = size == 8 and coefficients.shape[0] == 2 and retention.shape[0] == 4
        square = square and coefficients.shape[3] == 2 * TILE
        if square:
            return fused(coefficients, sky_year, hour_list, retention)
        return general(coefficients, sky_year, hour_list, retention)

    placed = (P("view", "patch", None, None), P("patch", None), P(), P("patch", None))
    return jax.shard_map(
        shards,
        mesh=mesh,
        in_specs=placed,
        out_specs=(P("patch", "view", None, None), P("patch", "view", None, None)),
        check_vma=False,
    )
```

```python
import jax
import jax.numpy as jnp
from jax import lax
from jax.experimental import pallas as pl
from jax.experimental.pallas import tpu as pltpu
from jax.sharding import PartitionSpec as P

binomial_taps = (0.0625, 0.25, 0.375, 0.25, 0.0625)
MESH = pl.DeviceIdType.MESH
LEVELS = 32767.0


def padded_2(block, sides, width):
    for axis, dim in sides:
        count = lax.axis_size(axis)
        forward = [(i, i + 1) for i in range(count - 1)]
        backward = [(target, source) for source, target in forward]
        low = lax.ppermute(
            lax.slice_in_dim(block, block.shape[dim] - width, None, axis=dim), axis, forward
        )
        high = lax.ppermute(lax.slice_in_dim(block, 0, width, axis=dim), axis, backward)
        block = jnp.concatenate([low, block, high], axis=dim)
    return block


def entering(value, axis, join, neutral, backward):
    count, mine = (lax.axis_size(axis), lax.axis_index(axis))
    pieces = jax.tree.map(lambda part: lax.all_gather(part, axis), value)
    if backward:
        pieces = jax.tree.map(lambda part: part[::-1], pieces)
        mine = count - 1 - mine
    running = jax.tree.map(
        lambda part, zero: jnp.full_like(part, 0) + jnp.asarray(zero, part.dtype), value, neutral
    )

    def hop(position, running):
        longer = join(running, jax.tree.map(lambda part: part[position], pieces))
        return jax.tree.map(lambda new, old: jnp.where(position < mine, new, old), longer, running)

    return lax.fori_loop(0, count - 1, hop, running)


def combine(earlier, later):
    return (earlier[0] * later[0], later[0] * earlier[1] + later[1])


def taps_sum(padded, axis, length):
    total = jnp.zeros(
        padded.shape[:axis] + (length,) + padded.shape[axis + 1 :],
        jnp.float32,
    )
    for offset in range(5):
        total = total + binomial_taps[offset] * lax.slice_in_dim(
            padded, offset, offset + length, axis=axis
        )
    return total


def general(coefficients, sky_year, hour_list, retention):
    sky_shard_values = jnp.take(sky_year, hour_list, axis=1)
    row_count = retention.shape[0]
    luminance = lax.psum_scatter(
        jnp.einsum(
            "ph,vprc->rvhc", sky_shard_values, coefficients, preferred_element_type=jnp.float32
        ),
        "patch",
        scatter_dimension=0,
        tiled=True,
    )
    padded = padded_2(luminance, (("patch", 0),), 2)
    image_width = padded.shape[3]
    wide_pad = jnp.pad(padded, ((0, 0), (0, 0), (0, 0), (2, 2)))
    across = taps_sum(wide_pad, 3, image_width)
    acuity = taps_sum(across, 0, row_count)
    retain_rates = retention[:, None, None, :]
    front_gain, front_sum = lax.associative_scan(combine, (retain_rates, luminance), axis=0)
    unity = (jnp.ones_like(front_gain[-1]), jnp.zeros_like(front_sum[-1]))
    _, incoming_down = entering((front_gain[-1], front_sum[-1]), "patch", combine, unity, False)
    forward = front_gain * incoming_down[None] + front_sum
    back_gain, back_sum = lax.associative_scan(
        combine, (retain_rates, luminance), reverse=True, axis=0
    )
    _, incoming_up = entering((back_gain[0], back_sum[0]), "patch", combine, unity, True)
    reverse_pass = back_gain * incoming_up[None] + back_sum
    veil = 0.125 * (forward + reverse_pass)
    return (acuity, veil)


TILE = 256
LANES = 128
GROUP = 4
SLOTS = 4


def encode(x):
    top = jnp.maximum(jnp.max(jnp.abs(x), axis=0, keepdims=True), 1e-30)
    level = jnp.round(x * (LEVELS / top))
    return level.astype(jnp.int32).astype(jnp.int16), top * (1.0 / LEVELS)


def decode(code, step):
    return code.astype(jnp.int32).astype(jnp.float32) * step


def kernel(
    sky_ref, coef_ref, ret_ref, acu_out, veil_out,
    lhs, held, mine, given, taken,
    code_out, top_out, code_in, top_in, lum, across,
    edge_out, edge_top_out, edge_in, edge_top_in, far_in, far_top_in,
    rets, gains, above, below, ends, acuity, veil,
    load_sem, ret_sem, pair_sem, hop_sem, edge_sem, far_sem, out_sem, local_sem,
):
    view = lax.axis_index("view")
    me = lax.axis_index("patch")
    devices = 8
    chips = 4
    core = me % 2
    chip = me // 2
    cx = chip % 2
    cy = chip // 2
    other = 1 - core
    partner = chip * 2 + other
    hours, depth = sky_ref.shape
    rows, _, columns = acuity.shape
    half = rows // 2
    tiles = columns // TILE
    strips = columns // LANES
    inner = TILE // LANES
    groups = rows // GROUP

    def at(target):
        return (view, target)

    def chip_of(k, owner):
        fx = (1 - owner) * (1 - k // 2) + owner * (1 - k % 2)
        fy = owner * (1 - k // 2) + (1 - owner) * (1 - k % 2)
        return 2 * (cy + fy * (1 - 2 * cy)) + cx + fx * (1 - 2 * cx)

    def remote(src, dst, send, recv, target):
        return pltpu.make_async_remote_copy(
            src_ref=src, dst_ref=dst, send_sem=send, recv_sem=recv,
            device_id=at(target), device_id_type=MESH,
        )

    units = [
        (0, 0, other), (0, 0, core), (1, 0, other), (1, 0, core),
        (2, 0, other), (2, 0, core), (0, 1, other), (0, 1, core),
        (1, 1, other), (1, 1, core), (2, 1, other), (2, 1, core),
        (3, 0, other), (3, 0, core), (3, 1, other), (3, 1, core),
    ]

    def load(u):
        k, t, v = units[u]
        slot = u % SLOTS
        return [
            pltpu.make_async_copy(
                coef_ref.at[v, :, chip_of(k, v), t * inner + j, s],
                held.at[slot, s, j],
                load_sem.at[slot, s * inner + j],
            )
            for s in range(groups)
            for j in range(inner)
        ]

    for u in range(SLOTS):
        for copy in load(u):
            copy.start()

    barrier = pltpu.get_barrier_semaphore()
    for step in range(1, devices):
        pl.semaphore_signal(
            barrier, inc=1, device_id=at((me + step) % devices), device_id_type=MESH
        )

    wide_shape = (depth, depth * GROUP)
    spread = (
        lax.broadcasted_iota(jnp.int32, wide_shape, 1) // GROUP
        == lax.broadcasted_iota(jnp.int32, wide_shape, 0)
    )
    wide = jnp.dot(
        sky_ref[...],
        jnp.where(spread, 1.0, 0.0).astype(jnp.bfloat16),
        preferred_element_type=jnp.float32,
    )
    place = lax.broadcasted_iota(jnp.int32, (hours, depth * GROUP), 1) % GROUP
    for r in range(GROUP):
        lhs[r * hours : (r + 1) * hours, :] = jnp.where(place == r, wide, 0.0).astype(jnp.bfloat16)

    rets[me] = ret_ref[...]

    def share(step):
        return remote(
            ret_ref, rets.at[me], ret_sem.at[0, step], ret_sem.at[1, step], (me + step) % devices
        )

    def pair(k, t):
        i = k * tiles + t
        return remote(
            given.at[k, pl.ds(t * inner, inner)], taken.at[k, pl.ds(t * inner, inner)],
            pair_sem.at[0, i], pair_sem.at[1, i], partner,
        )

    def run(u):
        k, t, v = units[u]
        slot = u % SLOTS
        dst = mine if u % 2 else given
        for copy in load(u):
            copy.wait()

        @pl.loop(0, groups, unroll=groups)
        def _(s):
            block = jnp.concatenate(
                [
                    held[slot, s, j].reshape(depth * GROUP, LANES)
                    for j in range(inner)
                ],
                axis=1,
            )
            image = jnp.dot(
                lhs[...], block, preferred_element_type=jnp.float32
            ).reshape(GROUP, hours, TILE)
            for j in range(inner):
                dst[k, t * inner + j, pl.ds(s * GROUP, GROUP)] = image[
                    :, :, j * LANES : (j + 1) * LANES
                ]

        if u == 0:
            pl.semaphore_wait(barrier, devices - 1)
        if u % 2 == 0:
            pair(k, t).start()
        if u + SLOTS < len(units):
            for copy in load(u + SLOTS):
                copy.start()

    def block(k, q):
        return k

    def hop(k, t):
        i = k * strips + t
        target = chip_of(block(max(k, 1), t), core) * 2 + core
        return [
            remote(code_out.at[k, t], code_in.at[k, t], hop_sem.at[0, 0, i], hop_sem.at[1, 0, i], target),
            remote(top_out.at[k, t], top_in.at[k, t], hop_sem.at[0, 1, i], hop_sem.at[1, 1, i], target),
        ]

    def first(k, q):
        n = block(k, q)

        @pl.loop(0, rows, unroll=rows)
        def _(r):
            code_out[k, q, r], top_out[k, q, r] = encode(mine[n, q, r] + taken[n, q, r])

        for copy in hop(k, q):
            copy.start()

    def second(q):
        n = block(2, q)

        for copy in hop(0, q):
            copy.wait_recv()

        @pl.loop(0, rows, unroll=rows)
        def _(r):
            came = decode(code_in[0, q, r], top_in[0, q, r])
            code_out[2, q, r], top_out[2, q, r] = encode(mine[n, q, r] + taken[n, q, r] + came)

        for copy in hop(2, q):
            copy.start()

    def gather(q):
        for copy in hop(1, q):
            copy.wait_recv()

        @pl.loop(0, rows, unroll=rows)
        def _(r):
            came = decode(code_in[1, q, r], top_in[1, q, r])
            mine[3, q, r] = mine[3, q, r] + taken[3, q, r] + came

    not_last = chip < chips - 1
    not_first = chip > 0

    def span(q):
        return pl.ds(q * LANES, LANES)

    def rate(r, q):
        return rets[chip * 2 + r // half, pl.ds(r % half, 1), span(q)]

    def edge(way, q):
        i = way * strips + q
        target = (chip + (1 - 2 * way) + chips) % chips * 2 + core
        return [
            remote(edge_out.at[way, q], edge_in.at[way, q], edge_sem.at[0, 0, i], edge_sem.at[1, 0, i], target),
            remote(edge_top_out.at[way, q], edge_top_in.at[way, q], edge_sem.at[0, 1, i], edge_sem.at[1, 1, i], target),
        ]

    def far(way, q, target, source):
        i = target * strips + q
        j = source * strips + q
        return [
            remote(edge_out.at[way, q, 2], far_in.at[source, q], far_sem.at[0, 0, i], far_sem.at[1, 0, j], target * 2 + core),
            remote(edge_top_out.at[way, q, 2], far_top_in.at[source, q], far_sem.at[0, 1, i], far_sem.at[1, 1, j], target * 2 + core),
        ]

    def keep(way, q, i, row):
        edge_out[way, q, i], edge_top_out[way, q, i] = encode(row)

    def each_target(q, act):
        for target in range(chips):
            @pl.when(target > chip + 1)
            def _():
                for copy in far(0, q, target, chip):
                    act(copy)

            @pl.when(target < chip - 1)
            def _():
                for copy in far(1, q, target, chip):
                    act(copy)

        @pl.when(not_last)
        def _():
            for copy in edge(0, q):
                act(copy)

        @pl.when(not_first)
        def _():
            for copy in edge(1, q):
                act(copy)

    def finish(q):
        for copy in hop(2, q):
            copy.wait_recv()

        state = jnp.zeros((hours, LANES), jnp.float32)
        for r in range(rows):
            row = mine[3, q, r] + decode(code_in[2, q, r], top_in[2, q, r])
            lum[r + 2, :, span(q)] = row
            state = rate(r, q) * state + row
            mine[0, q, r] = state
            if r < 2:
                keep(1, q, r, row)
            if r >= rows - 2:
                keep(0, q, r - (rows - 2), row)
        keep(0, q, 2, state)
        state = jnp.zeros((hours, LANES), jnp.float32)
        for r in range(rows - 1, -1, -1):
            state = rate(r, q) * state + lum[r + 2, :, span(q)]
            mine[0, q, r] = mine[0, q, r] + state
        keep(1, q, 2, state)
        each_target(q, lambda copy: copy.start())

    def prepare():
        for source in range(chips):
            total = None
            for r in range(rows):
                row = rets[source * 2 + r // half, r % half : r % half + 1, :]
                total = row if total is None else total * row
            gains[source] = total
        total = None
        for r in range(rows):
            row = rets[chip * 2 + r // half, r % half : r % half + 1, :]
            total = row if total is None else total * row
            above[r] = total
        total = None
        for r in range(rows - 1, -1, -1):
            row = rets[chip * 2 + r // half, r % half : r % half + 1, :]
            total = row if total is None else total * row
            below[r] = total

    def stay(q):
        return pltpu.make_async_copy(
            veil.at[pl.ds(core * half, half), :, span(q)],
            veil_out.at[:, core, :, span(q)],
            local_sem.at[1, q],
        )

    def leave(q):
        return remote(
            veil.at[pl.ds(other * half, half), :, span(q)],
            veil_out.at[:, core, :, span(q)],
            out_sem.at[0, 1, q],
            out_sem.at[1, 1, q],
            partner,
        )

    def glare(t):
        for source in range(chips):
            @pl.when((source < chip - 1) | (source > chip + 1))
            def _():
                for copy in far(0, t, source, source):
                    copy.wait_recv()

        ends[0] = jnp.zeros((hours, LANES), jnp.float32)
        ends[1] = jnp.zeros((hours, LANES), jnp.float32)

        @pl.when(not_first)
        def _():
            for copy in edge(0, t):
                copy.wait_recv()

        @pl.when(not_last)
        def _():
            for copy in edge(1, t):
                copy.wait_recv()

        for source in range(chips):
            @pl.when(source < chip - 1)
            def _():
                ends[0] = gains[source, :, span(t)] * ends[0] + decode(far_in[source, t], far_top_in[source, t])

            @pl.when(source == chip - 1)
            def _():
                ends[0] = gains[source, :, span(t)] * ends[0] + decode(edge_in[0, t, 2], edge_top_in[0, t, 2])

        for source in range(chips - 1, -1, -1):
            @pl.when(source > chip + 1)
            def _():
                ends[1] = gains[source, :, span(t)] * ends[1] + decode(far_in[source, t], far_top_in[source, t])

            @pl.when(source == chip + 1)
            def _():
                ends[1] = gains[source, :, span(t)] * ends[1] + decode(edge_in[1, t, 2], edge_top_in[1, t, 2])

        for r in range(rows):
            veil[r, :, span(t)] = 0.125 * (
                mine[0, t, r] + (above[r, :, span(t)] * ends[0] + below[r, :, span(t)] * ends[1])
            )
        stay(t).start()
        leave(t).start()

    column = lax.broadcasted_iota(jnp.int32, (hours, LANES), 1)

    def shifted(row, k):
        moved = pltpu.roll(row, (-k) % columns, 1)
        if k > 0:
            last = jnp.where(column < LANES - k, moved[:, columns - LANES :], 0.0)
            return jnp.concatenate([moved[:, : columns - LANES], last], axis=1)
        head = jnp.where(column >= -k, moved[:, :LANES], 0.0)
        return jnp.concatenate([head, moved[:, LANES:]], axis=1)

    def blur(row):
        return (
            binomial_taps[2] * row
            + binomial_taps[1] * (shifted(row, -1) + shifted(row, 1))
            + binomial_taps[0] * (shifted(row, -2) + shifted(row, 2))
        )

    def paired(k, t):
        pair(k, t).wait_recv()

    for u in range(3):
        run(u)
    paired(0, 0)
    first(0, 0)
    first(0, 1)
    for step in range(1, devices):
        share(step).start()
    run(3)
    run(4)
    paired(1, 0)
    first(1, 0)
    first(1, 1)
    run(5)
    run(6)
    paired(2, 0)
    second(0)
    run(7)
    second(1)
    run(8)
    paired(0, 1)
    first(0, 2)
    first(0, 3)
    run(9)
    run(10)
    paired(1, 1)
    first(1, 2)
    run(11)
    paired(2, 1)
    first(1, 3)
    for u in range(12, 16):
        run(u)
    for step in range(1, devices):
        share(step).wait()
    prepare()
    paired(3, 0)
    gather(0)
    gather(1)
    second(2)
    second(3)
    finish(0)
    finish(1)
    paired(3, 1)
    gather(2)
    gather(3)
    finish(2)
    glare(0)
    finish(3)
    glare(1)
    glare(2)

    def sharpen(outer):
        def rows_of(owner):
            source = 6 * owner if outer else 2 + 2 * owner
            target = 2 * owner if outer else 2 - 2 * owner
            return pl.ds(source, 2), pl.ds(target, 2)

        source, target = rows_of(core)
        sent, landed = rows_of(other)
        return [
            pltpu.make_async_copy(acuity.at[source], acu_out.at[target, core], local_sem.at[0, outer]),
            remote(
                acuity.at[sent], acu_out.at[landed, core],
                out_sem.at[0, 0, outer], out_sem.at[1, 0, outer], partner,
            ),
        ]

    @pl.loop(0, rows, unroll=2)
    def _(r):
        across[r] = blur(lum[r + 2])

    def down_taps(x0, x1, x2, x3, x4):
        return binomial_taps[2] * x2 + binomial_taps[1] * (x1 + x3) + binomial_taps[0] * (x0 + x4)

    @pl.loop(2, rows - 2)
    def _(r):
        acuity[r] = down_taps(*[across[r + k] for k in range(-2, 3)])

    for copy in sharpen(0):
        copy.start()

    zero = jnp.zeros((hours, columns), jnp.float32)

    def border(way, place):
        for i in range(2):
            row = jnp.concatenate(
                [decode(edge_in[way, q, i], edge_top_in[way, q, i]) for q in range(strips)], axis=1
            )
            lum[place + i] = blur(row)

    glare(3)

    @pl.when(not_first)
    def _():
        border(0, 0)

    @pl.when(chip == 0)
    def _():
        for i in range(2):
            lum[i] = zero

    @pl.when(not_last)
    def _():
        border(1, rows + 2)

    @pl.when(chip == chips - 1)
    def _():
        for i in range(2):
            lum[rows + 2 + i] = zero

    for r in (0, 1, rows - 2, rows - 1):
        acuity[r] = down_taps(
            *[
                across[s] if 0 <= s < rows else lum[s + 2]
                for s in range(r - 2, r + 3)
            ]
        )
    for copy in sharpen(1):
        copy.start()

    for k in range(chips):
        for t in range(tiles):
            pair(k, t).wait_send()
    for k in range(3):
        for q in range(strips):
            for copy in hop(k, q):
                copy.wait_send()
    for q in range(strips):
        each_target(q, lambda copy: copy.wait_send())
    for outer in range(2):
        for copy in sharpen(outer):
            copy.wait()
    for q in range(strips):
        stay(q).wait()
        leave(q).wait()


def fused(coefficients, sky_year, hour_list, retention):
    days = lax.broadcasted_iota(jnp.int32, (hour_list.shape[0], sky_year.shape[1]), 1)
    picks = (days == hour_list[:, None]).astype(jnp.bfloat16)
    sky = jnp.einsum(
        "hy,py->hp", picks, sky_year, preferred_element_type=jnp.float32
    ).astype(jnp.bfloat16)
    views, depth, all_rows, columns = coefficients.shape
    hours = hour_list.shape[0]
    half = retention.shape[0]
    rows = 2 * half
    chips = all_rows // rows
    groups = rows // GROUP
    tiles = columns // TILE
    strips = columns // LANES
    f32, bf16, i16 = jnp.float32, jnp.bfloat16, jnp.int16
    grouped = coefficients.reshape(
        views, depth, chips, groups, GROUP, columns // LANES, LANES
    ).transpose(0, 1, 2, 5, 3, 4, 6)
    image = (rows, hours, columns)
    tile = (strips, rows, hours, LANES)
    tops = (strips, rows, 1, LANES)
    out = jax.ShapeDtypeStruct((half, views, hours, columns), f32)
    dma = pltpu.SemaphoreType.DMA
    return pl.pallas_call(
        kernel,
        out_shape=(out, out),
        in_specs=[
            pl.BlockSpec(memory_space=pltpu.VMEM),
            pl.BlockSpec(memory_space=pl.ANY),
            pl.BlockSpec(memory_space=pltpu.VMEM),
        ],
        out_specs=[pl.BlockSpec(memory_space=pl.ANY)] * 2,
        scratch_shapes=[
            pltpu.VMEM((GROUP * hours, depth * GROUP), bf16),
            pltpu.VMEM((SLOTS, groups, TILE // LANES, depth, GROUP, LANES), bf16),
            pltpu.VMEM((chips,) + tile, f32),
            pltpu.VMEM((chips,) + tile, f32),
            pltpu.VMEM((chips,) + tile, f32),
            pltpu.VMEM((3,) + tile, i16),
            pltpu.VMEM((3,) + tops, f32),
            pltpu.VMEM((3,) + tile, i16),
            pltpu.VMEM((3,) + tops, f32),
            pltpu.VMEM((rows + 4, hours, columns), f32),
            pltpu.VMEM(image, f32),
            pltpu.VMEM((2, strips, 3, hours, LANES), i16),
            pltpu.VMEM((2, strips, 3, 1, LANES), f32),
            pltpu.VMEM((2, strips, 3, hours, LANES), i16),
            pltpu.VMEM((2, strips, 3, 1, LANES), f32),
            pltpu.VMEM((chips, strips, hours, LANES), i16),
            pltpu.VMEM((chips, strips, 1, LANES), f32),
            pltpu.VMEM((2 * chips, half, columns), f32),
            pltpu.VMEM((chips, 1, columns), f32),
            pltpu.VMEM((rows, 1, columns), f32),
            pltpu.VMEM((rows, 1, columns), f32),
            pltpu.VMEM((2, hours, LANES), f32),
            pltpu.VMEM(image, f32),
            pltpu.VMEM(image, f32),
            dma((SLOTS, groups * (TILE // LANES))),
            dma((2, 2 * chips)),
            dma((2, chips * tiles)),
            dma((2, 2, 3 * strips)),
            dma((2, 2, 2 * strips)),
            dma((2, 2, chips * strips)),
            dma((2, 2, strips)),
            dma((2, strips)),
        ],
        compiler_params=pltpu.CompilerParams(
            collective_id=0, has_side_effects=True, vmem_limit_bytes=46 * 1024 * 1024
        ),
    )(sky, grouped, retention)


def solution(mesh):
    size = mesh.shape["patch"]

    def shards(coefficients, sky_year, hour_list, retention):
        square = size == 8 and coefficients.shape[0] == 2 and retention.shape[0] == 4
        square = square and coefficients.shape[3] == 2 * TILE
        if square:
            return fused(coefficients, sky_year, hour_list, retention)
        return general(coefficients, sky_year, hour_list, retention)

    placed = (P("view", "patch", None, None), P("patch", None), P(), P("patch", None))
    return jax.shard_map(
        shards,
        mesh=mesh,
        in_specs=placed,
        out_specs=(P("patch", "view", None, None), P("patch", "view", None, None)),
        check_vma=False,
    )
```

```python
import jax
import jax.numpy as jnp
from jax import lax
from jax.experimental import pallas as pl
from jax.experimental.pallas import tpu as pltpu
from jax.sharding import PartitionSpec as P

binomial_taps = (0.0625, 0.25, 0.375, 0.25, 0.0625)
MESH = pl.DeviceIdType.MESH
LEVELS = 32767.0


def padded_2(block, sides, width):
    for axis, dim in sides:
        count = lax.axis_size(axis)
        forward = [(i, i + 1) for i in range(count - 1)]
        backward = [(target, source) for source, target in forward]
        low = lax.ppermute(
            lax.slice_in_dim(block, block.shape[dim] - width, None, axis=dim), axis, forward
        )
        high = lax.ppermute(lax.slice_in_dim(block, 0, width, axis=dim), axis, backward)
        block = jnp.concatenate([low, block, high], axis=dim)
    return block


def entering(value, axis, join, neutral, backward):
    count, mine = (lax.axis_size(axis), lax.axis_index(axis))
    pieces = jax.tree.map(lambda part: lax.all_gather(part, axis), value)
    if backward:
        pieces = jax.tree.map(lambda part: part[::-1], pieces)
        mine = count - 1 - mine
    running = jax.tree.map(
        lambda part, zero: jnp.full_like(part, 0) + jnp.asarray(zero, part.dtype), value, neutral
    )

    def hop(position, running):
        longer = join(running, jax.tree.map(lambda part: part[position], pieces))
        return jax.tree.map(lambda new, old: jnp.where(position < mine, new, old), longer, running)

    return lax.fori_loop(0, count - 1, hop, running)


def combine(earlier, later):
    return (earlier[0] * later[0], later[0] * earlier[1] + later[1])


def taps_sum(padded, axis, length):
    total = jnp.zeros(
        padded.shape[:axis] + (length,) + padded.shape[axis + 1 :],
        jnp.float32,
    )
    for offset in range(5):
        total = total + binomial_taps[offset] * lax.slice_in_dim(
            padded, offset, offset + length, axis=axis
        )
    return total


def general(coefficients, sky_year, hour_list, retention):
    sky_shard_values = jnp.take(sky_year, hour_list, axis=1)
    row_count = retention.shape[0]
    luminance = lax.psum_scatter(
        jnp.einsum(
            "ph,vprc->rvhc", sky_shard_values, coefficients, preferred_element_type=jnp.float32
        ),
        "patch",
        scatter_dimension=0,
        tiled=True,
    )
    padded = padded_2(luminance, (("patch", 0),), 2)
    image_width = padded.shape[3]
    wide_pad = jnp.pad(padded, ((0, 0), (0, 0), (0, 0), (2, 2)))
    across = taps_sum(wide_pad, 3, image_width)
    acuity = taps_sum(across, 0, row_count)
    retain_rates = retention[:, None, None, :]
    front_gain, front_sum = lax.associative_scan(combine, (retain_rates, luminance), axis=0)
    unity = (jnp.ones_like(front_gain[-1]), jnp.zeros_like(front_sum[-1]))
    _, incoming_down = entering((front_gain[-1], front_sum[-1]), "patch", combine, unity, False)
    forward = front_gain * incoming_down[None] + front_sum
    back_gain, back_sum = lax.associative_scan(
        combine, (retain_rates, luminance), reverse=True, axis=0
    )
    _, incoming_up = entering((back_gain[0], back_sum[0]), "patch", combine, unity, True)
    reverse_pass = back_gain * incoming_up[None] + back_sum
    veil = 0.125 * (forward + reverse_pass)
    return (acuity, veil)


TILE = 256
LANES = 128
GROUP = 4
SLOTS = 4


def encode(x):
    top = jnp.maximum(jnp.max(jnp.abs(x), axis=0, keepdims=True), 1e-30)
    level = jnp.round(x * (LEVELS / top))
    return level.astype(jnp.int32).astype(jnp.int16), top * (1.0 / LEVELS)


def decode(code, step):
    return code.astype(jnp.int32).astype(jnp.float32) * step


def kernel(
    sky_ref, coef_ref, ret_ref, acu_out, veil_out,
    lhs, held, mine, given, taken,
    code_out, top_out, code_in, top_in, lum, across,
    edge_out, edge_top_out, edge_in, edge_top_in, far_in, far_top_in,
    rets, gains, above, below, ends, acuity, veil,
    load_sem, ret_sem, pair_sem, hop_sem, edge_sem, far_sem, out_sem, local_sem,
):
    view = lax.axis_index("view")
    me = lax.axis_index("patch")
    devices = 8
    chips = 4
    core = me % 2
    chip = me // 2
    cx = chip % 2
    cy = chip // 2
    other = 1 - core
    partner = chip * 2 + other
    hours, depth = sky_ref.shape
    rows, _, columns = acuity.shape
    half = rows // 2
    tiles = columns // TILE
    strips = columns // LANES
    inner = TILE // LANES
    groups = rows // GROUP

    def at(target):
        return (view, target)

    def chip_of(k, owner):
        fx = (1 - owner) * (1 - k // 2) + owner * (1 - k % 2)
        fy = owner * (1 - k // 2) + (1 - owner) * (1 - k % 2)
        return 2 * (cy + fy * (1 - 2 * cy)) + cx + fx * (1 - 2 * cx)

    def remote(src, dst, send, recv, target):
        return pltpu.make_async_remote_copy(
            src_ref=src, dst_ref=dst, send_sem=send, recv_sem=recv,
            device_id=at(target), device_id_type=MESH,
        )

    units = [
        (0, 0, other), (0, 0, core), (1, 0, other), (1, 0, core),
        (2, 0, other), (2, 0, core), (0, 1, other), (0, 1, core),
        (1, 1, other), (1, 1, core), (2, 1, other), (2, 1, core),
        (3, 0, other), (3, 0, core), (3, 1, other), (3, 1, core),
    ]

    def load(u):
        k, t, v = units[u]
        slot = u % SLOTS
        return [
            pltpu.make_async_copy(
                coef_ref.at[v, :, chip_of(k, v), t * inner + j, s],
                held.at[slot, s, j],
                load_sem.at[slot, s * inner + j],
            )
            for s in range(groups)
            for j in range(inner)
        ]

    for u in range(SLOTS):
        for copy in load(u):
            copy.start()

    barrier = pltpu.get_barrier_semaphore()
    for step in range(1, devices):
        pl.semaphore_signal(
            barrier, inc=1, device_id=at((me + step) % devices), device_id_type=MESH
        )

    wide_shape = (depth, depth * GROUP)
    spread = (
        lax.broadcasted_iota(jnp.int32, wide_shape, 1) // GROUP
        == lax.broadcasted_iota(jnp.int32, wide_shape, 0)
    )
    wide = jnp.dot(
        sky_ref[...],
        jnp.where(spread, 1.0, 0.0).astype(jnp.bfloat16),
        preferred_element_type=jnp.float32,
    )
    place = lax.broadcasted_iota(jnp.int32, (hours, depth * GROUP), 1) % GROUP
    for r in range(GROUP):
        lhs[r * hours : (r + 1) * hours, :] = jnp.where(place == r, wide, 0.0).astype(jnp.bfloat16)

    rets[me] = ret_ref[...]

    def share(step):
        return remote(
            ret_ref, rets.at[me], ret_sem.at[0, step], ret_sem.at[1, step], (me + step) % devices
        )

    def pair(k, t):
        i = k * tiles + t
        return remote(
            given.at[k, pl.ds(t * inner, inner)], taken.at[k, pl.ds(t * inner, inner)],
            pair_sem.at[0, i], pair_sem.at[1, i], partner,
        )

    def run(u):
        k, t, v = units[u]
        slot = u % SLOTS
        dst = mine if u % 2 else given
        for copy in load(u):
            copy.wait()

        @pl.loop(0, groups, unroll=groups)
        def _(s):
            block = jnp.concatenate(
                [
                    held[slot, s, j].reshape(depth * GROUP, LANES)
                    for j in range(inner)
                ],
                axis=1,
            )
            image = jnp.dot(
                lhs[...], block, preferred_element_type=jnp.float32
            ).reshape(GROUP, hours, TILE)
            for j in range(inner):
                dst[k, t * inner + j, pl.ds(s * GROUP, GROUP)] = image[
                    :, :, j * LANES : (j + 1) * LANES
                ]

        if u == 0:
            pl.semaphore_wait(barrier, devices - 1)
        if u % 2 == 0:
            pair(k, t).start()
        if u + SLOTS < len(units):
            for copy in load(u + SLOTS):
                copy.start()

    def both(t):
        return pl.ds(t * inner, inner)

    def hop(k, t):
        i = k * tiles + t
        target = chip_of(max(k, 1), core) * 2 + core
        return [
            remote(dst_of.at[k, both(t)], in_of.at[k, both(t)], hop_sem.at[0, n, i], hop_sem.at[1, n, i], target)
            for n, (dst_of, in_of) in enumerate(((code_out, code_in), (top_out, top_in)))
        ]

    def start(copies):
        for copy in copies:
            copy.start()

    def arrived(copies):
        for copy in copies:
            copy.wait_recv()

    def first(k, q):
        @pl.loop(0, rows, unroll=rows)
        def _(r):
            code_out[k, q, r], top_out[k, q, r] = encode(mine[k, q, r] + taken[k, q, r])

        if q % inner == inner - 1:
            start(hop(k, q // inner))

    def second(q):
        if q % inner == 0:
            arrived(hop(0, q // inner))

        @pl.loop(0, rows, unroll=rows)
        def _(r):
            came = decode(code_in[0, q, r], top_in[0, q, r])
            code_out[2, q, r], top_out[2, q, r] = encode(mine[2, q, r] + taken[2, q, r] + came)

        if q % inner == inner - 1:
            start(hop(2, q // inner))

    def gather(q):
        if q % inner == 0:
            arrived(hop(1, q // inner))

        @pl.loop(0, rows, unroll=rows)
        def _(r):
            came = decode(code_in[1, q, r], top_in[1, q, r])
            mine[3, q, r] = mine[3, q, r] + taken[3, q, r] + came

    not_last = chip < chips - 1
    not_first = chip > 0

    def span(q):
        return pl.ds(q * LANES, LANES)

    def rate(r, q):
        return rets[chip * 2 + r // half, pl.ds(r % half, 1), span(q)]

    def edge(way, t):
        i = way * tiles + t
        target = (chip + (1 - 2 * way) + chips) % chips * 2 + core
        return [
            remote(edge_out.at[way, both(t)], edge_in.at[way, both(t)], edge_sem.at[0, 0, i], edge_sem.at[1, 0, i], target),
            remote(edge_top_out.at[way, both(t)], edge_top_in.at[way, both(t)], edge_sem.at[0, 1, i], edge_sem.at[1, 1, i], target),
        ]

    def far(way, t, target, source):
        i = target * tiles + t
        j = source * tiles + t
        return [
            remote(edge_out.at[way, both(t), 2], far_in.at[source, both(t)], far_sem.at[0, 0, i], far_sem.at[1, 0, j], target * 2 + core),
            remote(edge_top_out.at[way, both(t), 2], far_top_in.at[source, both(t)], far_sem.at[0, 1, i], far_sem.at[1, 1, j], target * 2 + core),
        ]

    def keep(way, q, i, row):
        edge_out[way, q, i], edge_top_out[way, q, i] = encode(row)

    def each_target(q, act):
        for target in range(chips):
            @pl.when(target > chip + 1)
            def _():
                for copy in far(0, q, target, chip):
                    act(copy)

            @pl.when(target < chip - 1)
            def _():
                for copy in far(1, q, target, chip):
                    act(copy)

        @pl.when(not_last)
        def _():
            for copy in edge(0, q):
                act(copy)

        @pl.when(not_first)
        def _():
            for copy in edge(1, q):
                act(copy)

    def finish(q):
        if q % inner == 0:
            arrived(hop(2, q // inner))

        state = jnp.zeros((hours, LANES), jnp.float32)
        for r in range(rows):
            row = mine[3, q, r] + decode(code_in[2, q, r], top_in[2, q, r])
            lum[r + 2, :, span(q)] = row
            state = rate(r, q) * state + row
            mine[0, q, r] = state
            if r < 2:
                keep(1, q, r, row)
            if r >= rows - 2:
                keep(0, q, r - (rows - 2), row)
        keep(0, q, 2, state)
        state = jnp.zeros((hours, LANES), jnp.float32)
        for r in range(rows - 1, -1, -1):
            state = rate(r, q) * state + lum[r + 2, :, span(q)]
            mine[0, q, r] = mine[0, q, r] + state
        keep(1, q, 2, state)
        if q % inner == inner - 1:
            each_target(q // inner, lambda copy: copy.start())

    def prepare():
        for source in range(chips):
            total = None
            for r in range(rows):
                row = rets[source * 2 + r // half, r % half : r % half + 1, :]
                total = row if total is None else total * row
            gains[source] = total
        total = None
        for r in range(rows):
            row = rets[chip * 2 + r // half, r % half : r % half + 1, :]
            total = row if total is None else total * row
            above[r] = total
        total = None
        for r in range(rows - 1, -1, -1):
            row = rets[chip * 2 + r // half, r % half : r % half + 1, :]
            total = row if total is None else total * row
            below[r] = total

    def stay(q):
        return pltpu.make_async_copy(
            veil.at[pl.ds(core * half, half), :, span(q)],
            veil_out.at[:, core, :, span(q)],
            local_sem.at[1, q],
        )

    def leave(q):
        return remote(
            veil.at[pl.ds(other * half, half), :, span(q)],
            veil_out.at[:, core, :, span(q)],
            out_sem.at[0, 1, q],
            out_sem.at[1, 1, q],
            partner,
        )

    def met(t):
        for source in range(chips):
            @pl.when((source < chip - 1) | (source > chip + 1))
            def _():
                arrived(far(0, t, source, source))

        @pl.when(not_first)
        def _():
            arrived(edge(0, t))

        @pl.when(not_last)
        def _():
            arrived(edge(1, t))

    def glare(t):
        if t % inner == 0:
            met(t // inner)
        ends[0] = jnp.zeros((hours, LANES), jnp.float32)
        ends[1] = jnp.zeros((hours, LANES), jnp.float32)

        for source in range(chips):
            @pl.when(source < chip - 1)
            def _():
                ends[0] = gains[source, :, span(t)] * ends[0] + decode(far_in[source, t], far_top_in[source, t])

            @pl.when(source == chip - 1)
            def _():
                ends[0] = gains[source, :, span(t)] * ends[0] + decode(edge_in[0, t, 2], edge_top_in[0, t, 2])

        for source in range(chips - 1, -1, -1):
            @pl.when(source > chip + 1)
            def _():
                ends[1] = gains[source, :, span(t)] * ends[1] + decode(far_in[source, t], far_top_in[source, t])

            @pl.when(source == chip + 1)
            def _():
                ends[1] = gains[source, :, span(t)] * ends[1] + decode(edge_in[1, t, 2], edge_top_in[1, t, 2])

        for r in range(rows):
            veil[r, :, span(t)] = 0.125 * (
                mine[0, t, r] + (above[r, :, span(t)] * ends[0] + below[r, :, span(t)] * ends[1])
            )
        stay(t).start()
        leave(t).start()

    column = lax.broadcasted_iota(jnp.int32, (hours, LANES), 1)

    def shifted(row, k):
        moved = pltpu.roll(row, (-k) % columns, 1)
        if k > 0:
            last = jnp.where(column < LANES - k, moved[:, columns - LANES :], 0.0)
            return jnp.concatenate([moved[:, : columns - LANES], last], axis=1)
        head = jnp.where(column >= -k, moved[:, :LANES], 0.0)
        return jnp.concatenate([head, moved[:, LANES:]], axis=1)

    def blur(row):
        return (
            binomial_taps[2] * row
            + binomial_taps[1] * (shifted(row, -1) + shifted(row, 1))
            + binomial_taps[0] * (shifted(row, -2) + shifted(row, 2))
        )

    def paired(k, t):
        pair(k, t).wait_recv()

    for u in range(3):
        run(u)
    paired(0, 0)
    first(0, 0)
    first(0, 1)
    for step in range(1, devices):
        share(step).start()
    run(3)
    run(4)
    paired(1, 0)
    first(1, 0)
    first(1, 1)
    run(5)
    run(6)
    run(7)
    run(8)
    paired(0, 1)
    first(0, 2)
    first(0, 3)
    run(9)
    paired(2, 0)
    second(0)
    second(1)
    run(10)
    paired(1, 1)
    first(1, 2)
    first(1, 3)
    run(11)
    paired(2, 1)
    for u in range(12, 16):
        run(u)
    for step in range(1, devices):
        share(step).wait()
    prepare()
    paired(3, 0)
    gather(0)
    gather(1)
    second(2)
    second(3)
    finish(0)
    finish(1)
    paired(3, 1)
    gather(2)
    gather(3)
    finish(2)
    finish(3)
    glare(0)
    glare(1)

    def sharpen(outer):
        def rows_of(owner):
            source = 6 * owner if outer else 2 + 2 * owner
            target = 2 * owner if outer else 2 - 2 * owner
            return pl.ds(source, 2), pl.ds(target, 2)

        source, target = rows_of(core)
        sent, landed = rows_of(other)
        return [
            pltpu.make_async_copy(acuity.at[source], acu_out.at[target, core], local_sem.at[0, outer]),
            remote(
                acuity.at[sent], acu_out.at[landed, core],
                out_sem.at[0, 0, outer], out_sem.at[1, 0, outer], partner,
            ),
        ]

    @pl.loop(0, rows, unroll=2)
    def _(r):
        across[r] = blur(lum[r + 2])

    def down_taps(x0, x1, x2, x3, x4):
        return binomial_taps[2] * x2 + binomial_taps[1] * (x1 + x3) + binomial_taps[0] * (x0 + x4)

    @pl.loop(2, rows - 2)
    def _(r):
        acuity[r] = down_taps(*[across[r + k] for k in range(-2, 3)])

    for copy in sharpen(0):
        copy.start()

    zero = jnp.zeros((hours, columns), jnp.float32)

    def border(way, place):
        for i in range(2):
            row = jnp.concatenate(
                [decode(edge_in[way, q, i], edge_top_in[way, q, i]) for q in range(strips)], axis=1
            )
            lum[place + i] = blur(row)

    glare(2)
    glare(3)

    @pl.when(not_first)
    def _():
        border(0, 0)

    @pl.when(chip == 0)
    def _():
        for i in range(2):
            lum[i] = zero

    @pl.when(not_last)
    def _():
        border(1, rows + 2)

    @pl.when(chip == chips - 1)
    def _():
        for i in range(2):
            lum[rows + 2 + i] = zero

    for r in (0, 1, rows - 2, rows - 1):
        acuity[r] = down_taps(
            *[
                across[s] if 0 <= s < rows else lum[s + 2]
                for s in range(r - 2, r + 3)
            ]
        )
    for copy in sharpen(1):
        copy.start()

    for k in range(chips):
        for t in range(tiles):
            pair(k, t).wait_send()
    for t in range(tiles):
        for k in range(3):
            for copy in hop(k, t):
                copy.wait_send()
        each_target(t, lambda copy: copy.wait_send())
    for outer in range(2):
        for copy in sharpen(outer):
            copy.wait()
    for q in range(strips):
        stay(q).wait()
        leave(q).wait()


def fused(coefficients, sky_year, hour_list, retention):
    days = lax.broadcasted_iota(jnp.int32, (hour_list.shape[0], sky_year.shape[1]), 1)
    picks = (days == hour_list[:, None]).astype(jnp.bfloat16)
    sky = jnp.einsum(
        "hy,py->hp", picks, sky_year, preferred_element_type=jnp.float32
    ).astype(jnp.bfloat16)
    views, depth, all_rows, columns = coefficients.shape
    hours = hour_list.shape[0]
    half = retention.shape[0]
    rows = 2 * half
    chips = all_rows // rows
    groups = rows // GROUP
    tiles = columns // TILE
    strips = columns // LANES
    f32, bf16, i16 = jnp.float32, jnp.bfloat16, jnp.int16
    grouped = coefficients.reshape(
        views, depth, chips, groups, GROUP, columns // LANES, LANES
    ).transpose(0, 1, 2, 5, 3, 4, 6)
    image = (rows, hours, columns)
    tile = (strips, rows, hours, LANES)
    tops = (strips, rows, 1, LANES)
    out = jax.ShapeDtypeStruct((half, views, hours, columns), f32)
    dma = pltpu.SemaphoreType.DMA
    return pl.pallas_call(
        kernel,
        out_shape=(out, out),
        in_specs=[
            pl.BlockSpec(memory_space=pltpu.VMEM),
            pl.BlockSpec(memory_space=pl.ANY),
            pl.BlockSpec(memory_space=pltpu.VMEM),
        ],
        out_specs=[pl.BlockSpec(memory_space=pl.ANY)] * 2,
        scratch_shapes=[
            pltpu.VMEM((GROUP * hours, depth * GROUP), bf16),
            pltpu.VMEM((SLOTS, groups, TILE // LANES, depth, GROUP, LANES), bf16),
            pltpu.VMEM((chips,) + tile, f32),
            pltpu.VMEM((chips,) + tile, f32),
            pltpu.VMEM((chips,) + tile, f32),
            pltpu.VMEM((3,) + tile, i16),
            pltpu.VMEM((3,) + tops, f32),
            pltpu.VMEM((3,) + tile, i16),
            pltpu.VMEM((3,) + tops, f32),
            pltpu.VMEM((rows + 4, hours, columns), f32),
            pltpu.VMEM(image, f32),
            pltpu.VMEM((2, strips, 3, hours, LANES), i16),
            pltpu.VMEM((2, strips, 3, 1, LANES), f32),
            pltpu.VMEM((2, strips, 3, hours, LANES), i16),
            pltpu.VMEM((2, strips, 3, 1, LANES), f32),
            pltpu.VMEM((chips, strips, hours, LANES), i16),
            pltpu.VMEM((chips, strips, 1, LANES), f32),
            pltpu.VMEM((2 * chips, half, columns), f32),
            pltpu.VMEM((chips, 1, columns), f32),
            pltpu.VMEM((rows, 1, columns), f32),
            pltpu.VMEM((rows, 1, columns), f32),
            pltpu.VMEM((2, hours, LANES), f32),
            pltpu.VMEM(image, f32),
            pltpu.VMEM(image, f32),
            dma((SLOTS, groups * (TILE // LANES))),
            dma((2, 2 * chips)),
            dma((2, chips * tiles)),
            dma((2, 2, 3 * strips)),
            dma((2, 2, 2 * strips)),
            dma((2, 2, chips * strips)),
            dma((2, 2, strips)),
            dma((2, strips)),
        ],
        compiler_params=pltpu.CompilerParams(
            collective_id=0, has_side_effects=True, vmem_limit_bytes=46 * 1024 * 1024
        ),
    )(sky, grouped, retention)


def solution(mesh):
    size = mesh.shape["patch"]

    def shards(coefficients, sky_year, hour_list, retention):
        square = size == 8 and coefficients.shape[0] == 2 and retention.shape[0] == 4
        square = square and coefficients.shape[3] == 2 * TILE
        if square:
            return fused(coefficients, sky_year, hour_list, retention)
        return general(coefficients, sky_year, hour_list, retention)

    placed = (P("view", "patch", None, None), P("patch", None), P(), P("patch", None))
    return jax.shard_map(
        shards,
        mesh=mesh,
        in_specs=placed,
        out_specs=(P("patch", "view", None, None), P("patch", "view", None, None)),
        check_vma=False,
    )
```
